256 devices in a mesh: section: 4 (over x), owner: 64 (over z, y, core).
Axes of the slice: x: 4, y: 4, z: 8, core: 2. Of those that a mesh axis runs over, the one named last changes fastest.
Arguments:
- probe_values: bfloat16 [8, 524288, 128], P('section', 'owner'), may hold values from -6 to 6
- probe_keys: int32 [8, 524288], P('section', 'owner'), may hold values from 0 to 2047
- group_ids: int32 [8, 524288], P('section', 'owner'), may hold values from 0 to 1023
- block_dest: int32 [8, 4096, 1], P('section', 'owner'), may hold values from 0 to 63; in each aligned block of 64 rows (0 to 63, 64 to 127, ..., all dimensions but the last counted through in order) at most 2 rows name the same one
- filter_bits: int32 [4, 8, 32768], P('section', None, 'owner'), may hold values from 0 to 65535, as said below
- section_weights: bfloat16 [4, 128, 128], P('section'), may hold values from -0.5 to 0.5
- build_keys: int32 [262144], P('owner'), may hold values from 0 to 2047
- build_values: bfloat16 [262144, 128], P('owner'), may hold values from -6 to 6
Outputs:
- group_sums: float32 [1024, 128], P(('section', 'owner'))
The draws below stay inside these ranges and needn't reach their ends.
Inputs may be any that keep to these rules, and one draw needn't show every extreme that they name: `block_dest`: in each micro-batch, no owner is named by more than 2 of the 64 blocks of one device, a bound that some block reaches. `filter_bits`: bit b of a word is the keep bit of row 16 w + b; the upper bits are 0.
All inputs are finite; a program needn't handle non-finite values.
Results may differ from the reference program's by a relative error of at most 0.012.
Values may be sent and summed in bfloat16 or wider, within the bound.
A program may use at most 128 MiB of HBM per device.

```python
import math
import jax
import jax.numpy as jnp
import numpy as np

P_SIZE = 128
BLOCK = 128
CAP = 2
MBS = 2
KEYS_OWN = 2048
BUILD_OWN = 4096
MB = 8
NB = 64
ROWS = 524288
WORDS = 32768
BUILD = 262144
GROUPS = 1024
N_SECTION = 4
N_OWNER = 64


def draw_filter_bits(key, part):
    lower_bits = jax.random.randint(jax.random.fold_in(key, 11), (N_SECTION, MB, WORDS), 0, 65536, dtype=jnp.int32)
    upper_bits = jax.random.randint(jax.random.fold_in(key, 12), (N_SECTION, MB, WORDS), 0, 65536, dtype=jnp.int32)
    return lower_bits | upper_bits


def set_ends(result, own_key, smallest, largest):
    index_at = [jax.random.randint(jax.random.fold_in(own_key, axis), (), 0, length) for axis, length in enumerate(result.shape)]
    main_axis = result.shape.index(max(result.shape))
    next_to = index_at[:main_axis] + [(index_at[main_axis] + 1) % result.shape[main_axis]] + index_at[main_axis + 1:]
    return result.at[tuple(index_at)].set(smallest).at[tuple(next_to)].set(largest)


def levels(key, extent, pieces, smallest, high):
    def one(position, shards_of):
        heights = jax.random.uniform(jax.random.fold_in(jax.random.fold_in(key, 6), position), (shards_of,), jnp.float32, smallest / len(pieces), high / len(pieces))
        return jnp.repeat(jnp.exp(heights), extent[position] // shards_of).reshape((-1,) + (1,) * (len(extent) - position - 1))

    gain = one(*pieces[0])
    for cut in pieces[1:]:
        gain = gain * one(*cut)
    return gain


def deal_out(rng, own, number, rows, amount, top, bound, lean):
    sequence = jax.random.permutation(rng, amount)
    heavy_load, ordinary = portions_of(amount, rows * top, bound, lean, True), portions_of(amount, rows * top, bound, lean, False)
    places = jnp.arange(amount)

    def named(sizes, offset_by):
        used = int((sizes > 0).sum())
        fixed = max(1, used // 4)
        passed = fixed + (places - fixed + offset_by * (used - fixed)) % max(1, amount - fixed)
        return jnp.zeros((amount,), jnp.int32).at[sequence[jnp.where(places < fixed, places, passed)]].set(jnp.asarray(sizes, jnp.int32))

    sizes = jnp.where(number % 4 == 0, named(heavy_load, number // 4), named(ordinary, number - number // 4 - 1))
    mixed = jax.random.permutation(jax.random.fold_in(own, 3), amount)
    donor, receiver = mixed[0:amount // 2 * 2:2], mixed[1:amount // 2 * 2:2]
    room = jnp.minimum(sizes[donor] - 1, bound - sizes[receiver]) // 2
    room = jnp.where((donor == sequence[0]) | (receiver == sequence[0]) | (sizes[receiver] == 0), 0, jnp.maximum(room, 0))
    passed = jax.random.randint(jax.random.fold_in(own, 4), (amount // 2,), 0, 1 << 20) % (room + 1)
    sizes = sizes.at[donor].add(-passed).at[receiver].add(passed)
    items = jnp.searchsorted(jnp.cumsum(sizes), jnp.arange(rows * top), side="right").astype(jnp.int32)
    grid = items.reshape(top, rows).T
    grid = grid[jax.random.permutation(jax.random.fold_in(own, 1), rows)]
    offset_by = jax.random.randint(jax.random.fold_in(own, 2), (rows, 1), 0, top)
    return jnp.take_along_axis(grid, (jnp.arange(top)[None, :] + offset_by) % top, axis=1)


def portions_of(amount, total, most, lean, full):
    portions = [(1 << 20) // math.isqrt(standing ** lean) + 1 for standing in range(1, amount + 1)]
    largest = most if full else min(most, max(-(-total // amount), total * portions[0] // sum(portions)))
    least = 1 if total - largest >= amount - 1 else 0
    counts, spare = [largest] + [least] * (amount - 1), total - largest - least * (amount - 1)
    while spare > 0:
        candidates = [i for i in range(1, amount) if counts[i] < largest] or [i for i in range(1, amount) if counts[i] < most]
        mass, remaining = sum([portions[i] for i in candidates]), spare
        for i in candidates:
            extra = min(most - counts[i], max(1, remaining * portions[i] // mass), spare)
            counts[i] = counts[i] + extra
            spare = spare - extra
    return np.array(counts)


def centred(stream_key, extent, scale, most, shards=(), kind=jnp.bfloat16):
    entries = jax.random.normal(stream_key, extent, jnp.float32) * scale
    if len(shards) > 0:
        entries = levels(stream_key, extent, shards, -0.22, 0.18) * entries
    return jnp.clip(entries, min=-most, max=most).astype(kind)


def setup_inputs(seed: int = 0) -> dict:
    arg_keys = jax.random.split(jax.random.key(seed), 9)
    probe_values = centred(arg_keys[0], (MB, ROWS, P_SIZE), 1.0, 6.0, ((0, 4), (1, 64)))
    probe_keys = set_ends(jax.random.randint(arg_keys[1], (MB, ROWS), 0, KEYS_OWN), jax.random.fold_in(arg_keys[1], 1), 0, KEYS_OWN - 1).astype(jnp.int32)
    group_ids = set_ends(jax.random.randint(arg_keys[2], (MB, ROWS), 0, GROUPS), jax.random.fold_in(arg_keys[2], 1), 0, GROUPS - 1).astype(jnp.int32)
    block_dest_keys = jax.random.split(jax.random.fold_in(arg_keys[3], 1), MB * (NB * N_OWNER) // NB)
    block_dest_turns = jax.random.permutation(jax.random.fold_in(arg_keys[3], 3), MB * (NB * N_OWNER) // NB)
    block_dest = jax.vmap(lambda own, number: deal_out(jax.random.fold_in(arg_keys[3], 2), own, number, NB, N_OWNER, 1, CAP, 2))(block_dest_keys, block_dest_turns).reshape((MB, NB * N_OWNER, 1))
    filter_bits = draw_filter_bits(jax.random.fold_in(arg_keys[8], 71), 0)
    section_weights = centred(arg_keys[5], (N_SECTION, P_SIZE, P_SIZE), P_SIZE ** -0.5, 0.5, ((0, 4),))
    build_keys = set_ends(jax.random.randint(arg_keys[6], (BUILD,), 0, KEYS_OWN), jax.random.fold_in(arg_keys[6], 1), 0, KEYS_OWN - 1).astype(jnp.int32)
    build_values = centred(arg_keys[7], (BUILD, P_SIZE), 1.0, 6.0, ((0, 64),))
    return dict(probe_values=probe_values, probe_keys=probe_keys, group_ids=group_ids, block_dest=block_dest, filter_bits=filter_bits, section_weights=section_weights, build_keys=build_keys, build_values=build_values)


def unpack_bits(bit_words):
    shifts = jnp.arange(16, dtype=jnp.int32)
    spread = jnp.right_shift(bit_words[..., None], shifts) & 1
    return spread.reshape(bit_words.shape[:-1] + (bit_words.shape[-1] * 16,)).astype(jnp.float32)


def apply_section(payload, kept_mask, weight):
    columns = payload.shape[-1]
    projected = jnp.dot(payload.reshape(-1, columns), weight, preferred_element_type=jnp.float32)
    projected = projected.reshape(payload.shape)
    updated = kept_mask[..., None] * (payload.astype(jnp.float32) + jax.nn.silu(projected))
    return updated.astype(jnp.bfloat16)


def reference(probe_values, probe_keys, group_ids, block_dest, filter_bits, section_weights, build_keys, build_values):
    owners = (jnp.arange(N_OWNER * BUILD_OWN, dtype=jnp.int32) // BUILD_OWN).astype(jnp.int32)
    key_table = jax.ops.segment_sum(build_values.astype(jnp.float32), owners * KEYS_OWN + build_keys.astype(jnp.int32), num_segments=N_OWNER * KEYS_OWN)
    group_sums = jnp.zeros((GROUPS, P_SIZE), jnp.float32)
    for micro in range(MB):
        home_section = micro // MBS
        payload = probe_values[micro]
        for step_number in range(N_SECTION):
            section_at = (home_section + step_number) % N_SECTION
            kept_mask = unpack_bits(filter_bits[section_at, micro])
            payload = apply_section(payload, kept_mask, section_weights[section_at])
        dest_rows = jnp.repeat(block_dest[micro, :, 0], BLOCK).astype(jnp.int32)
        matched = jnp.take(key_table, dest_rows * KEYS_OWN + probe_keys[micro].astype(jnp.int32), axis=0)
        joined = (payload.astype(jnp.float32) * matched).astype(jnp.bfloat16)
        group_sums = group_sums + jax.ops.segment_sum(joined.astype(jnp.float32), group_ids[micro].astype(jnp.int32), num_segments=GROUPS)
    return group_sums
```

```python
import functools

import jax
import jax.numpy as jnp
from jax import lax
from jax.experimental import pallas as pl
from jax.experimental.pallas import tpu as pltpu
from jax.sharding import Mesh
from jax.sharding import PartitionSpec as P

OWNER = ("owner_0", "owner_1", "owner_2")
AXES = ("section", "owner_0", "owner_1", "owner_2")
MESH = pl.DeviceIdType.MESH
F32 = jnp.float32
BF16 = jnp.bfloat16
ROWS = 16384
COLS = 32
CHUNK = 1024
NCHUNK = ROWS // CHUNK
BUILD = 4096
AUX = 168
NT = (((1,), (1,)), ((), ()))


def remote(src, dst, ssem, rsem, dev):
    return pltpu.make_async_remote_copy(
        src_ref=src, dst_ref=dst, send_sem=ssem, recv_sem=rsem, device_id=dev, device_id_type=MESH
    )


def silu_add(v, u):
    h = 0.5 * u
    return (v + (h + h * jnp.tanh(h))).astype(BF16)


def build_table(s, bk_ref, bv_ref, store):
    sel = lax.broadcasted_iota(jnp.int32, (COLS, 128), 1) == (
        lax.broadcasted_iota(jnp.int32, (COLS, 128), 0) + s * COLS
    )
    sel = sel.astype(F32).astype(BF16)
    total = jnp.zeros((256, 256), F32)
    step = 1024
    for i in range(BUILD // step):
        vals = lax.dot_general(sel, bv_ref[pl.ds(i * step, step), :], NT, preferred_element_type=F32)
        key = bk_ref[:, pl.ds(i * step, step)]
        low = (key & 255).astype(F32).astype(BF16)
        high = key >> 8
        hot = jnp.where(
            lax.broadcasted_iota(jnp.int32, (256, step), 0).astype(F32).astype(BF16) == low,
            jnp.ones((), BF16),
            jnp.zeros((), BF16),
        )
        wide = jnp.concatenate([jnp.where(high == p, vals, 0.0) for p in range(8)], axis=0)
        total += lax.dot_general(wide.astype(BF16), hot, NT, preferred_element_type=F32)
    store(total.astype(BF16))


def delta(e):
    return ((e + 1) // 2) * (2 * (e % 2) - 1)


def move_kernel(
    w_ref, v_ref, bk_ref, bv_ref, aux_ref, rbuf, tabs, auxg,
    sendbuf, wbuf, last, ws, wr, xs, xr, zs, zr, ys, yr, ls, lr, cs, cr, ps, pr, own_sem,
):
    s, z, y, c = [lax.axis_index(a) for a in AXES]

    def xdev(d):
        return (lax.rem(s + d, 4), z, y, c)

    def zdev(e):
        return (s, lax.rem(z + 8 + delta(e), 8), y, c)

    def ydev(d):
        return (s, z, lax.rem(y + 4 + d, 4), c)

    pair = (s, z, y, 1 - c)
    barrier = pltpu.get_barrier_semaphore()
    for d in (1, 2, 3):
        pl.semaphore_signal(barrier, inc=1, device_id=xdev(d), device_id_type=MESH)
    for e in range(1, 8):
        pl.semaphore_signal(barrier, inc=1, device_id=zdev(e), device_id_type=MESH)
    for d in (-1, 1):
        pl.semaphore_signal(barrier, inc=1, device_id=ydev(d), device_id_type=MESH)
    pl.semaphore_signal(barrier, inc=1, device_id=pair, device_id_type=MESH)
    pl.semaphore_wait(barrier, 13)

    def wcopy(d):
        return remote(w_ref, wbuf.at[s], ws.at[d], wr.at[d], xdev(d))

    def xcopy(d):
        return remote(aux_ref, auxg.at[s], xs.at[d], xr.at[d], xdev(d))

    def zfrom(e):
        return lax.rem(z + 8 - delta(e), 8)

    def zcopy(e):
        here = tabs.at[c, z, y]
        return remote(here, here, zs.at[e], zr.at[e], zdev(e))

    def ycopy(k, e):
        here = tabs.at[c, zfrom(e), y]
        return remote(here, here, ys.at[k, e], yr.at[k, e], ydev(1 - 2 * k))

    def lcopy(e):
        sign = 1 - 2 * (e % 2)
        here = tabs.at[c, zfrom(e), lax.rem(y + 4 - sign, 4)]
        return remote(here, here, ls.at[e], lr.at[e], ydev(sign))

    def ccopy(k, e):
        at = (0, -1, 1, 2)[k]
        here = tabs.at[c, zfrom(e), lax.rem(y + 4 + at, 4)]
        return remote(here, here, cs.at[k, e], cr.at[k, e], pair)

    def carrive(k, e):
        at = (0, -1, 1, 2)[k]
        here = tabs.at[1 - c, zfrom(e), lax.rem(y + 4 + at, 4)]
        return remote(here, here, cs.at[k, e], cr.at[k, e], pair)

    def pcopy(d, i):
        at = pl.ds(pl.multiple_of(i * CHUNK, CHUNK), CHUNK)
        return remote(
            sendbuf.at[lax.rem(s + d, 4), :, at], rbuf.at[s, :, at], ps.at[d, i], pr.at[d, i], xdev(d)
        )

    for d in (1, 3, 2):
        wcopy(d).start()
    for d in (1, 3, 2):
        xcopy(d).start()
    own_aux = pltpu.make_async_copy(aux_ref, auxg.at[s], own_sem.at[0])
    own_aux.start()
    own_w = pltpu.make_async_copy(w_ref, wbuf.at[s], own_sem.at[1])
    own_w.start()

    def put_table(value):
        tabs[c, z, y] = value

    build_table(s, bk_ref, bv_ref, put_table)

    own_w.wait()
    for d in (1, 2, 3):
        wcopy(d).wait_recv()
    w_last = wbuf[lax.rem(s + 3, 4)].astype(F32).T.astype(BF16)
    last[pl.ds(0, 128), :] = w_last
    eye = lax.broadcasted_iota(jnp.int32, (128, 128), 0) == lax.broadcasted_iota(jnp.int32, (128, 128), 1)
    last[pl.ds(128, 128), :] = eye.astype(F32).astype(BF16)

    def sections(i):
        at = pl.ds(pl.multiple_of(i * CHUNK, CHUNK), CHUNK)
        v = v_ref[at, :]
        for j in range(3):
            u = jnp.dot(v, wbuf[lax.rem(s + j, 4)], preferred_element_type=F32)
            v = silu_add(v.astype(F32), u)
        out = lax.dot_general(last[...], v, NT, preferred_element_type=F32)
        v = silu_add(out[128:], out[:128])
        for q in range(4):
            sendbuf[q, :, at] = v[q * COLS : (q + 1) * COLS]

    sections(0)
    for e in range(1, 8):
        zcopy(e).start()
    for k in (0, 1):
        ycopy(k, 0).start()
    ccopy(0, 0).start()

    def step(i, carry):
        sections(i)
        for d in (1, 3, 2):
            pcopy(d, i - 1).start()

        @pl.when((i >= 2) & (i % 2 == 0))
        def _():
            e = i // 2
            zcopy(e).wait_recv()
            for k in (0, 1):
                ycopy(k, e).start()
            ccopy(0, e).start()

        return carry

    lax.fori_loop(1, NCHUNK, step, 0)
    own_p = pltpu.make_async_copy(sendbuf.at[s], rbuf.at[s], own_sem.at[2])
    own_p.start()
    for d in (1, 3, 2):
        pcopy(d, NCHUNK - 1).start()

    def near(e, carry):
        ycopy(0, e).wait_recv()
        ycopy(1, e).wait_recv()
        lcopy(e).start()
        ccopy(1, e).start()
        ccopy(2, e).start()
        return carry

    lax.fori_loop(0, 8, near, 0)

    def far(e, carry):
        lcopy(e).wait_recv()
        ccopy(3, e).start()
        return carry

    lax.fori_loop(0, 8, far, 0)

    def finish(e, carry):
        for k in range(4):
            carrive(k, e).wait_recv()
            ccopy(k, e).wait_send()
        for k in (0, 1):
            ycopy(k, e).wait_send()
        lcopy(e).wait_send()
        return carry

    lax.fori_loop(0, 8, finish, 0)

    def finish_z(e, carry):
        zcopy(e).wait_send()
        return carry

    lax.fori_loop(1, 8, finish_z, 0)

    def finish_p(i, carry):
        for d in (1, 2, 3):
            pcopy(d, i).wait()
        return carry

    lax.fori_loop(0, NCHUNK, finish_p, 0)
    for d in (1, 2, 3):
        wcopy(d).wait_send()
        xcopy(d).wait()
    own_aux.wait()
    own_p.wait()


def move(w, v, bk, bv, aux):
    dma = pltpu.SemaphoreType.DMA
    vmem = pl.BlockSpec(memory_space=pltpu.VMEM)
    return pl.pallas_call(
        move_kernel,
        name="move",
        out_shape=(
            jax.ShapeDtypeStruct((4, COLS, ROWS), BF16),
            jax.ShapeDtypeStruct((2, 8, 4, 256, 256), BF16),
            jax.ShapeDtypeStruct((4, AUX, 128), jnp.int32),
        ),
        in_specs=[vmem] * 5,
        out_specs=(vmem, vmem, vmem),
        scratch_shapes=[
            pltpu.VMEM((4, COLS, ROWS), BF16),
            pltpu.VMEM((4, 128, 128), BF16),
            pltpu.VMEM((256, 128), BF16),
            dma((4,)), dma((4,)), dma((4,)), dma((4,)),
            dma((8,)), dma((8,)),
            dma((2, 8)), dma((2, 8)), dma((8,)), dma((8,)),
            dma((4, 8)), dma((4, 8)),
            dma((4, NCHUNK)), dma((4, NCHUNK)),
            dma((3,)),
        ],
        compiler_params=pltpu.CompilerParams(
            collective_id=0, has_side_effects=True, vmem_limit_bytes=60 << 20
        ),
    )(w, v, bk, bv, aux)


def join_kernel(where_ref, code_ref, pay_ref, tab_ref, acc_ref):
    i = pl.program_id(0)

    @pl.when(i == 0)
    def _():
        acc_ref[...] = jnp.zeros_like(acc_ref)

    one, zero = jnp.ones((), BF16), jnp.zeros((), BF16)
    code = code_ref[0]
    low = (code & 255).astype(F32).astype(BF16)
    high = (code >> 8) & 7
    glow = (code >> 11) & 7
    ghigh = (code >> 14).astype(F32).astype(BF16)
    rows256 = lax.broadcasted_iota(jnp.int32, (256, 128), 0).astype(F32).astype(BF16)
    rows128 = lax.broadcasted_iota(jnp.int32, (128, 128), 0).astype(F32).astype(BF16)
    wide, hots = [], []
    for b in range(CHUNK // 128):
        at = slice(b * 128, (b + 1) * 128)
        hot = jnp.where(rows256 == low[:, at], one, zero)
        table = tab_ref[where_ref[i * (CHUNK // 128) + b]]
        out = jnp.dot(table, hot, preferred_element_type=F32)
        matched = jnp.zeros((COLS, 128), F32)
        for p in range(8):
            matched = jnp.where(high[:, at] == p, out[p * COLS : (p + 1) * COLS], matched)
        joined = pay_ref[0, :, at].astype(F32) * matched
        wide.append(
            jnp.concatenate(
                [jnp.where(glow[:, at] == p, joined, 0.0).astype(BF16) for p in range(8)], axis=0
            )
        )
        hots.append(jnp.where(rows128 == ghigh[:, at], one, zero))
    acc_ref[...] += lax.dot_general(
        jnp.concatenate(hots, axis=1), jnp.concatenate(wide, axis=1), NT, preferred_element_type=F32
    )


def join(where, code, pay, tabs):
    n = 4 * NCHUNK
    return pl.pallas_call(
        join_kernel,
        name="join",
        out_shape=jax.ShapeDtypeStruct((128, 256), F32),
        grid_spec=pltpu.PrefetchScalarGridSpec(
            num_scalar_prefetch=1,
            grid=(n,),
            in_specs=[
                pl.BlockSpec((1, 1, CHUNK), lambda i, w: (i, 0, 0)),
                pl.BlockSpec((1, COLS, CHUNK), lambda i, w: (i // NCHUNK, 0, i % NCHUNK)),
                pl.BlockSpec((64, 256, 256), lambda i, w: (0, 0, 0), pipeline_mode=pl.Buffered(1)),
            ],
            out_specs=pl.BlockSpec((128, 256), lambda i, w: (0, 0)),
        ),
        compiler_params=pltpu.CompilerParams(
            dimension_semantics=("arbitrary",), vmem_limit_bytes=40 << 20
        ),
    )(where, code, pay, tabs)


def reduce_kernel(acc_ref, out_ref, first, mid, second, s1, r1, s2, r2):
    s, z, y, c = [lax.axis_index(a) for a in AXES]
    me = s * 2 + c
    place = z * 4 + y

    def peer1(k):
        t = lax.rem(me + k, 8)
        return t // 2, lax.rem(t, 2)

    def dev2(k):
        t = lax.rem(place + k, 32)
        return (s, t // 4, lax.rem(t, 4), c)

    barrier = pltpu.get_barrier_semaphore()
    for k in range(1, 8):
        ps, pc = peer1(k)
        pl.semaphore_signal(barrier, inc=1, device_id=(ps, z, y, pc), device_id_type=MESH)

    def greet(k, carry):
        pl.semaphore_signal(barrier, inc=1, device_id=dev2(k), device_id_type=MESH)
        return carry

    lax.fori_loop(1, 32, greet, 0)
    pl.semaphore_wait(barrier, 38)

    def piece(ps, pc):
        return (
            pl.ds(pl.multiple_of(ps * 32, 32), 32),
            pl.ds(pl.multiple_of(pc * 128, 128), 128),
        )

    def copy1(k):
        ps, pc = peer1(k)
        rows, lanes = piece(ps, pc)
        return remote(acc_ref.at[rows, lanes], first.at[me], s1.at[k], r1.at[k], (ps, z, y, pc))

    def copy2(k):
        return remote(
            mid.at[lax.rem(place + k, 32)], second.at[place], s2.at[k], r2.at[k], dev2(k)
        )

    for k in range(1, 8):
        copy1(k).start()
    rows, lanes = piece(s, c)
    first[me] = acc_ref[rows, lanes]
    for k in range(1, 8):
        copy1(k).wait_recv()
    for x in range(4):
        mid[:, x, :] = first[2 * x] + first[2 * x + 1]

    def send(k, carry):
        copy2(k).start()
        return carry

    lax.fori_loop(1, 32, send, 0)
    second[place] = mid[place]

    def take(k, carry):
        copy2(k).wait_recv()
        return carry

    lax.fori_loop(1, 32, take, 0)
    out_ref[...] = jnp.sum(second[...], axis=0)
    for k in range(1, 8):
        copy1(k).wait_send()

    def done(k, carry):
        copy2(k).wait_send()
        return carry

    lax.fori_loop(1, 32, done, 0)


def reduce_all(acc):
    dma = pltpu.SemaphoreType.DMA
    vmem = pl.BlockSpec(memory_space=pltpu.VMEM)
    return pl.pallas_call(
        reduce_kernel,
        name="reduce_all",
        out_shape=jax.ShapeDtypeStruct((4, 128), F32),
        in_specs=[vmem],
        out_specs=vmem,
        scratch_shapes=[
            pltpu.VMEM((8, 32, 128), F32),
            pltpu.VMEM((32, 4, 128), F32),
            pltpu.VMEM((32, 4, 128), F32),
            dma((8,)), dma((8,)), dma((32,)), dma((32,)),
        ],
        compiler_params=pltpu.CompilerParams(
            collective_id=1, has_side_effects=True, vmem_limit_bytes=16 << 20
        ),
    )(acc)


def local(probe_values, probe_keys, group_ids, block_dest, filter_bits, section_weights, build_keys, build_values):
    code = (probe_keys | (group_ids << 11)).reshape(128, 128)
    aux = jnp.concatenate(
        [
            code,
            filter_bits.reshape(32, 128),
            jnp.broadcast_to(block_dest.reshape(1, 128), (8, 128)),
        ],
        axis=0,
    )
    rbuf, tabs, auxg = move(
        section_weights[0], probe_values.reshape(ROWS, 128), build_keys.reshape(1, BUILD), build_values, aux
    )
    bits = auxg[:, 128:160].reshape(4, 8, 512)
    bits = bits[0] & bits[1] & bits[2] & bits[3]
    kept = (bits[..., None] >> jnp.arange(16, dtype=jnp.int32)) & 1
    code = auxg[:, :128].reshape(4 * NCHUNK, 1, CHUNK)
    code = jnp.where(kept.reshape(code.shape) == 1, code, code | (1 << 21))
    dest = auxg[:, 160].reshape(512)
    where = (dest & 1) * 32 + (dest >> 3) * 4 + ((dest >> 1) & 3)
    acc = join(where, code, rbuf, tabs.reshape(64, 256, 256))
    out = reduce_all(acc)
    return out.reshape(4, 4, COLS).transpose(1, 0, 2).reshape(4, 128)


def solution(mesh):
    torus = Mesh(mesh.devices.reshape(mesh.shape["section"], 8, 4, 2), AXES)
    return jax.shard_map(
        local,
        mesh=torus,
        in_specs=(
            P("section", OWNER, None),
            P("section", OWNER),
            P("section", OWNER),
            P("section", OWNER, None),
            P("section", None, OWNER),
            P("section", None, None),
            P(OWNER),
            P(OWNER, None),
        ),
        out_specs=P(AXES, None),
        check_vma=False,
    )
```

```python
import functools

import jax
import jax.numpy as jnp
from jax import lax
from jax.experimental import pallas as pl
from jax.experimental.pallas import tpu as pltpu
from jax.sharding import Mesh
from jax.sharding import PartitionSpec as P

OWNER = ("owner_0", "owner_1", "owner_2")
AXES = ("section", "owner_0", "owner_1", "owner_2")
MESH = pl.DeviceIdType.MESH
F32 = jnp.float32
BF16 = jnp.bfloat16
ROWS = 16384
COLS = 32
CHUNK = 1024
NCHUNK = ROWS // CHUNK
BUILD = 4096
NT = (((1,), (1,)), ((), ()))


def remote(src, dst, ssem, rsem, dev):
    return pltpu.make_async_remote_copy(
        src_ref=src, dst_ref=dst, send_sem=ssem, recv_sem=rsem, device_id=dev, device_id_type=MESH
    )


def silu_add(v, u):
    h = 0.5 * u
    return (v + (h + h * jnp.tanh(h))).astype(BF16)


def build_table(s, bk_ref, bv_ref, store):
    sel = lax.broadcasted_iota(jnp.int32, (COLS, 128), 1) == (
        lax.broadcasted_iota(jnp.int32, (COLS, 128), 0) + s * COLS
    )
    sel = sel.astype(F32).astype(BF16)
    total = jnp.zeros((256, 256), F32)
    step = 1024
    for i in range(BUILD // step):
        vals = lax.dot_general(sel, bv_ref[pl.ds(i * step, step), :], NT, preferred_element_type=F32)
        key = bk_ref[:, pl.ds(i * step, step)]
        low = (key & 255).astype(F32).astype(BF16)
        high = key >> 8
        hot = jnp.where(
            lax.broadcasted_iota(jnp.int32, (256, step), 0).astype(F32).astype(BF16) == low,
            jnp.ones((), BF16),
            jnp.zeros((), BF16),
        )
        wide = jnp.concatenate([jnp.where(high == p, vals, 0.0) for p in range(8)], axis=0)
        total += lax.dot_general(wide.astype(BF16), hot, NT, preferred_element_type=F32)
    store(total.astype(BF16))


def delta(e):
    return ((e + 1) // 2) * (2 * (e % 2) - 1)


def fused_kernel(
    w_ref, v_hbm, key_ref, grp_ref, dst_ref, bit_ref, bk_ref, bv_ref, out_ref,
    vbuf, sendbuf, rbuf, tabs, wbuf, last, codes, codeg, bitg, dests, destg, where_ref, kept_ref,
    hot0, hot1, wide0, wide1, acc_ref, first, mid, second,
    vs, ws, wr, xs, xr, zs, zr, ys, yr, ls, lr, cs, cr, ps, pr, own_sem, s1, r1, s2, r2,
):
    s, z, y, c = [lax.axis_index(a) for a in AXES]
    me = s * 2 + c
    place = z * 4 + y

    def xdev(d):
        return (lax.rem(s + d, 4), z, y, c)

    def zdev(e):
        return (s, lax.rem(z + 8 + delta(e), 8), y, c)

    def ydev(d):
        return (s, z, lax.rem(y + 4 + d, 4), c)

    pair = (s, z, y, 1 - c)

    def peer1(k):
        t = lax.rem(me + k, 8)
        return t // 2, lax.rem(t, 2)

    def dev2(k):
        t = lax.rem(place + k, 32)
        return (s, t // 4, lax.rem(t, 4), c)

    barrier = pltpu.get_barrier_semaphore()
    for k in range(1, 8):
        px, pc = peer1(k)
        pl.semaphore_signal(barrier, inc=1, device_id=(px, z, y, pc), device_id_type=MESH)

    def greet(k, carry):
        pl.semaphore_signal(barrier, inc=1, device_id=dev2(k), device_id_type=MESH)
        return carry

    lax.fori_loop(1, 32, greet, 0)

    def vcopy(i):
        at = pl.ds(pl.multiple_of(i * CHUNK, CHUNK), CHUNK)
        return pltpu.make_async_copy(v_hbm.at[at, :], vbuf.at[at, :], vs.at[i])

    def vstart(i, carry):
        vcopy(i).start()
        return carry

    lax.fori_loop(0, NCHUNK, vstart, 0)

    for i in range(NCHUNK):
        at = slice((i % 8) * CHUNK, (i % 8 + 1) * CHUNK)
        m = slice(i // 8, i // 8 + 1)
        codes[i : i + 1, :] = key_ref[m, at] | (grp_ref[m, at] << 11)
    d = dst_ref[...]
    dests[...] = jnp.zeros_like(dests)
    dests[0:2, 0:64] = (d & 1) * 32 + (d >> 3) * 4 + ((d >> 1) & 3)

    def wcopy(d):
        return remote(w_ref, wbuf.at[s], ws.at[d], wr.at[d], xdev(d))

    def xcopies(d):
        return [
            remote(a, b.at[s], xs.at[n, d], xr.at[n, d], xdev(d))
            for n, (a, b) in enumerate(((codes, codeg), (bit_ref, bitg), (dests, destg)))
        ]

    def slot(cc, zz, yy):
        return cc * 32 + zz * 4 + yy

    def zfrom(e):
        return lax.rem(z + 8 - delta(e), 8)

    def zcopy(e):
        here = tabs.at[slot(c, z, y)]
        return remote(here, here, zs.at[e], zr.at[e], zdev(e))

    def ycopy(k, e):
        here = tabs.at[slot(c, zfrom(e), y)]
        return remote(here, here, ys.at[k, e], yr.at[k, e], ydev(1 - 2 * k))

    def lcopy(e):
        sign = 1 - 2 * (e % 2)
        here = tabs.at[slot(c, zfrom(e), lax.rem(y + 4 - sign, 4))]
        return remote(here, here, ls.at[e], lr.at[e], ydev(sign))

    def ccopy(k, e):
        at = (0, -1, 1, 2)[k]
        here = tabs.at[slot(c, zfrom(e), lax.rem(y + 4 + at, 4))]
        return remote(here, here, cs.at[k, e], cr.at[k, e], pair)

    def carrive(k, e):
        at = (0, -1, 1, 2)[k]
        here = tabs.at[slot(1 - c, zfrom(e), lax.rem(y + 4 + at, 4))]
        return remote(here, here, cs.at[k, e], cr.at[k, e], pair)

    def pcopy(d, i):
        at = pl.ds(pl.multiple_of(i * CHUNK, CHUNK), CHUNK)
        return remote(
            sendbuf.at[lax.rem(s + d, 4), :, at], rbuf.at[s, :, at], ps.at[d, i], pr.at[d, i], xdev(d)
        )

    def put_table(value):
        tabs[slot(c, z, y)] = value

    build_table(s, bk_ref, bv_ref, put_table)
    pl.semaphore_wait(barrier, 38)

    for d in (1, 3, 2):
        wcopy(d).start()
    for e in range(1, 8):
        zcopy(e).start()
    for k in (0, 1):
        ycopy(k, 0).start()
    ccopy(0, 0).start()
    for d in (1, 3, 2):
        for cp in xcopies(d):
            cp.start()
    own = [
        pltpu.make_async_copy(a, b.at[s], own_sem.at[n])
        for n, (a, b) in enumerate(((codes, codeg), (bit_ref, bitg), (dests, destg), (w_ref, wbuf)))
    ]
    for cp in own:
        cp.start()
    for cp in own:
        cp.wait()
    for d in (1, 2, 3):
        wcopy(d).wait_recv()
    w_last = wbuf[lax.rem(s + 3, 4)].astype(F32).T.astype(BF16)
    last[pl.ds(0, 128), :] = w_last
    eye = lax.broadcasted_iota(jnp.int32, (128, 128), 0) == lax.broadcasted_iota(jnp.int32, (128, 128), 1)
    last[pl.ds(128, 128), :] = eye.astype(F32).astype(BF16)

    def sections(i):
        at = pl.ds(pl.multiple_of(i * CHUNK, CHUNK), CHUNK)
        vcopy(i).wait()
        v = vbuf[at, :]
        for j in range(3):
            u = jnp.dot(v, wbuf[lax.rem(s + j, 4)], preferred_element_type=F32)
            v = silu_add(v.astype(F32), u)
        out = lax.dot_general(last[...], v, NT, preferred_element_type=F32)
        v = silu_add(out[128:], out[:128])
        for q in range(4):
            sendbuf[q, :, at] = v[q * COLS : (q + 1) * COLS]

    sections(0)

    def step(i, carry):
        sections(i)
        for d in (1, 3, 2):
            pcopy(d, i - 1).start()

        @pl.when(i % 2 == 1)
        def _():
            @pl.when(i < 14)
            def _():
                e = i // 2 + 1
                zcopy(e).wait_recv()
                for k in (0, 1):
                    ycopy(k, e).start()
                ccopy(0, e).start()

        return carry

    lax.fori_loop(1, NCHUNK, step, 0)
    own_p = pltpu.make_async_copy(sendbuf.at[s], rbuf.at[s], own_sem.at[4])
    own_p.start()
    for d in (1, 3, 2):
        pcopy(d, NCHUNK - 1).start()

    for d in (1, 2, 3):
        for cp in xcopies(d):
            cp.wait_recv()
    to_scalar = pltpu.make_async_copy(destg, where_ref, own_sem.at[5])
    to_scalar.start()
    words = bitg[0] & bitg[1] & bitg[2] & bitg[3]
    parts = jnp.concatenate([words & 255, words >> 8], axis=0).astype(F32).astype(BF16)
    shift = lax.broadcasted_iota(jnp.int32, (8, CHUNK), 1) & 15
    wide_iota = lax.broadcasted_iota(jnp.int32, (512, CHUNK), 1) >> 4
    word_iota = lax.broadcasted_iota(jnp.int32, (512, CHUNK), 0)
    for k in range(8):
        spread = (wide_iota + k * 64 == word_iota).astype(F32).astype(BF16)
        got = jnp.dot(parts, spread, preferred_element_type=F32).astype(jnp.int32)
        kept_ref[k] = ((got[:8] + got[8:] * 256) >> shift) & 1
    to_scalar.wait()
    own_p.wait()
    acc_ref[...] = jnp.zeros_like(acc_ref)
    hot1[...] = jnp.zeros_like(hot1)
    wide1[...] = jnp.zeros_like(wide1)

    def near(e, carry):
        ycopy(0, e).wait_recv()
        ycopy(1, e).wait_recv()
        lcopy(e).start()
        ccopy(1, e).start()
        ccopy(2, e).start()
        return carry

    lax.fori_loop(0, 8, near, 0)

    def far(e, carry):
        lcopy(e).wait_recv()
        ccopy(3, e).start()
        return carry

    lax.fori_loop(0, 8, far, 0)

    def finish(e, carry):
        for k in range(4):
            carrive(k, e).wait_recv()
        return carry

    lax.fori_loop(0, 8, finish, 0)

    one, zero = jnp.ones((), BF16), jnp.zeros((), BF16)
    rows256 = lax.broadcasted_iota(jnp.int32, (256, 128), 0).astype(F32).astype(BF16)
    rows128 = lax.broadcasted_iota(jnp.int32, (128, 128), 0).astype(F32).astype(BF16)

    def gather(src, i, hot_ref, wide_ref):
        code = codeg[src, pl.ds(i, 1), :]
        kept = kept_ref[i % 8, pl.ds(2 * src + i // 8, 1), :]
        low = (code & 255).astype(F32).astype(BF16)
        high = (code >> 8) & 7
        glow = (code >> 11) & 7
        ghigh = jnp.where(kept == 1, code >> 14, -1).astype(F32).astype(BF16)
        for b in range(CHUNK // 128):
            at = slice(b * 128, (b + 1) * 128)
            hot = jnp.where(rows256 == low[:, at], one, zero)
            table = tabs[where_ref[src, i // 8, (i % 8) * 8 + b]]
            out = jnp.dot(table, hot, preferred_element_type=F32)
            matched = jnp.zeros((COLS, 128), F32)
            for p in range(8):
                matched = jnp.where(high[:, at] == p, out[p * COLS : (p + 1) * COLS], matched)
            pay = rbuf[src, :, pl.ds(pl.multiple_of(i * CHUNK + b * 128, 128), 128)]
            joined = pay.astype(F32) * matched
            for p in range(8):
                wide_ref[p * COLS : (p + 1) * COLS, at] = jnp.where(glow[:, at] == p, joined, 0.0).astype(BF16)
            hot_ref[:, at] = jnp.where(rows128 == ghigh[:, at], one, zero)

    def group(hot_ref, wide_ref):
        acc_ref[...] += lax.dot_general(hot_ref[...], wide_ref[...], NT, preferred_element_type=F32)

    def join(t, carry):
        d = t % 4
        i = t // 4 * 2
        src = lax.rem(s + 4 - d, 4)

        @pl.when(d > 0)
        def _():
            pcopy(d, i).wait_recv()
            pcopy(d, i + 1).wait_recv()

        group(hot1, wide1)
        gather(src, i, hot0, wide0)
        group(hot0, wide0)
        gather(src, i + 1, hot1, wide1)
        return carry

    lax.fori_loop(0, 32, join, 0)
    group(hot1, wide1)

    def piece(px, pc):
        return (
            pl.ds(pl.multiple_of(px * 32, 32), 32),
            pl.ds(pl.multiple_of(pc * 128, 128), 128),
        )

    def copy1(k):
        px, pc = peer1(k)
        rows, lanes = piece(px, pc)
        return remote(acc_ref.at[rows, lanes], first.at[me], s1.at[k], r1.at[k], (px, z, y, pc))

    def copy2(k):
        return remote(mid.at[lax.rem(place + k, 32)], second.at[place], s2.at[k], r2.at[k], dev2(k))

    for k in range(1, 8):
        copy1(k).start()
    rows, lanes = piece(s, c)
    first[me] = acc_ref[rows, lanes]

    def sent_e(e, carry):
        for k in range(4):
            ccopy(k, e).wait_send()
        for k in (0, 1):
            ycopy(k, e).wait_send()
        lcopy(e).wait_send()
        return carry

    lax.fori_loop(0, 8, sent_e, 0)

    def sent_z(e, carry):
        zcopy(e).wait_send()
        return carry

    lax.fori_loop(1, 8, sent_z, 0)

    def sent_p(i, carry):
        for d in (1, 2, 3):
            pcopy(d, i).wait_send()
        return carry

    lax.fori_loop(0, NCHUNK, sent_p, 0)
    for d in (1, 2, 3):
        wcopy(d).wait_send()
        for cp in xcopies(d):
            cp.wait_send()

    for k in range(1, 8):
        copy1(k).wait_recv()
    for x in range(4):
        mid[:, x, :] = first[2 * x] + first[2 * x + 1]

    def send(k, carry):
        copy2(k).start()
        return carry

    lax.fori_loop(1, 32, send, 0)
    second[place] = mid[place]

    def take(k, carry):
        copy2(k).wait_recv()
        return carry

    lax.fori_loop(1, 32, take, 0)
    total = jnp.sum(second[...], axis=0)
    for x in range(4):
        for k in range(4):
            out_ref[k : k + 1, x * COLS : (x + 1) * COLS] = total[x : x + 1, k * COLS : (k + 1) * COLS]
    for k in range(1, 8):
        copy1(k).wait_send()

    def done(k, carry):
        copy2(k).wait_send()
        return carry

    lax.fori_loop(1, 32, done, 0)


def local(probe_values, probe_keys, group_ids, block_dest, filter_bits, section_weights, build_keys, build_values):
    dma = pltpu.SemaphoreType.DMA
    vmem = pl.BlockSpec(memory_space=pltpu.VMEM)
    i32 = jnp.int32
    return pl.pallas_call(
        fused_kernel,
        name="fused",
        out_shape=jax.ShapeDtypeStruct((4, 128), F32),
        in_specs=[vmem, pl.BlockSpec(memory_space=pl.ANY)] + [vmem] * 6,
        out_specs=vmem,
        scratch_shapes=[
            pltpu.VMEM((ROWS, 128), BF16),
            pltpu.VMEM((4, COLS, ROWS), BF16),
            pltpu.VMEM((4, COLS, ROWS), BF16),
            pltpu.VMEM((64, 256, 256), BF16),
            pltpu.VMEM((4, 128, 128), BF16),
            pltpu.VMEM((256, 128), BF16),
            pltpu.VMEM((NCHUNK, CHUNK), i32),
            pltpu.VMEM((4, NCHUNK, CHUNK), i32),
            pltpu.VMEM((4, 8, 512), i32),
            pltpu.VMEM((8, 128), i32),
            pltpu.VMEM((4, 8, 128), i32),
            pltpu.SMEM((4, 8, 128), i32),
            pltpu.VMEM((8, 8, CHUNK), i32),
            pltpu.VMEM((128, CHUNK), BF16),
            pltpu.VMEM((128, CHUNK), BF16),
            pltpu.VMEM((256, CHUNK), BF16),
            pltpu.VMEM((256, CHUNK), BF16),
            pltpu.VMEM((128, 256), F32),
            pltpu.VMEM((8, 32, 128), F32),
            pltpu.VMEM((32, 4, 128), F32),
            pltpu.VMEM((32, 4, 128), F32),
            dma((NCHUNK,)),
            dma((4,)), dma((4,)), dma((3, 4)), dma((3, 4)),
            dma((8,)), dma((8,)),
            dma((2, 8)), dma((2, 8)), dma((8,)), dma((8,)),
            dma((4, 8)), dma((4, 8)),
            dma((4, NCHUNK)), dma((4, NCHUNK)),
            dma((6,)),
            dma((8,)), dma((8,)), dma((32,)), dma((32,)),
        ],
        compiler_params=pltpu.CompilerParams(
            collective_id=0, has_side_effects=True, vmem_limit_bytes=60 << 20
        ),
    )(
        section_weights[0],
        probe_values.reshape(ROWS, 128),
        probe_keys,
        group_ids,
        block_dest.reshape(2, 64),
        filter_bits[0],
        build_keys.reshape(1, BUILD),
        build_values,
    )


def solution(mesh):
    torus = Mesh(mesh.devices.reshape(mesh.shape["section"], 8, 4, 2), AXES)
    return jax.shard_map(
        local,
        mesh=torus,
        in_specs=(
            P("section", OWNER, None),
            P("section", OWNER),
            P("section", OWNER),
            P("section", OWNER, None),
            P("section", None, OWNER),
            P("section", None, None),
            P(OWNER),
            P(OWNER, None),
        ),
        out_specs=P(AXES, None),
        check_vma=False,
    )
```

```python
import functools

import jax
import jax.numpy as jnp
from jax import lax
from jax.experimental import pallas as pl
from jax.experimental.pallas import tpu as pltpu
from jax.sharding import Mesh
from jax.sharding import PartitionSpec as P

OWNER = ("owner_0", "owner_1", "owner_2")
AXES = ("section", "owner_0", "owner_1", "owner_2")
MESH = pl.DeviceIdType.MESH
F32 = jnp.float32
BF16 = jnp.bfloat16
ROWS = 16384
COLS = 32
CHUNK = 1024
NCHUNK = ROWS // CHUNK
BUILD = 4096
PERMUTED = 4
A_ROWS = 176
HOPS = (4, 3)
EVENTS = (None, (0, 1), (1, 1), (0, 2), (1, 2), (0, 3), (1, 3), (0, 4))
NT = (((1,), (1,)), ((), ()))


def remote(src, dst, ssem, rsem, dev):
    return pltpu.make_async_remote_copy(
        src_ref=src, dst_ref=dst, send_sem=ssem, recv_sem=rsem, device_id=dev, device_id_type=MESH
    )


def silu_add(v, h):
    return (v + (h + h * jnp.tanh(h))).astype(BF16)


def build_table(s, bk_ref, bv_ref, store):
    sel = lax.broadcasted_iota(jnp.int32, (COLS, 128), 1) == (
        lax.broadcasted_iota(jnp.int32, (COLS, 128), 0) + s * COLS
    )
    sel = sel.astype(F32).astype(BF16)
    total = jnp.zeros((256, 256), F32)
    step = 1024
    for i in range(BUILD // step):
        vals = lax.dot_general(sel, bv_ref[pl.ds(i * step, step), :], NT, preferred_element_type=F32)
        key = bk_ref[:, pl.ds(i * step, step)]
        low = (key & 255).astype(F32).astype(BF16)
        high = key >> 8
        hot = jnp.where(
            lax.broadcasted_iota(jnp.int32, (256, step), 0).astype(F32).astype(BF16) == low,
            jnp.ones((), BF16),
            jnp.zeros((), BF16),
        )
        wide = jnp.concatenate([jnp.where(high == p, vals, 0.0) for p in range(8)], axis=0)
        total += lax.dot_general(wide.astype(BF16), hot, NT, preferred_element_type=F32)
    store(total.astype(BF16))


def fused_kernel(
    w_ref, v_hbm, key_ref, grp_ref, dst_ref, bit_ref, bk_ref, bv_ref, out_ref,
    vbuf, sendbuf, rbuf, tabs, wbuf, half, last, codes, codeg, bitg, dests, destg, where_ref, kept_ref,
    acc_ref, first, mid, second,
    vs, ws, wr, xs, xr, azs, azr, bzs, bzr, bys, byr, ys, yr, ls, lr, cs, cr, cbs, cbr, ps, pr, own_sem, s1, r1, s2, r2,
):
    s, z, y, c = [lax.axis_index(a) for a in AXES]
    me = s * 2 + c
    place = z * 4 + y

    def xdev(d):
        return (lax.rem(s + d, 4), z, y, c)

    def ydev(d):
        return (s, z, lax.rem(y + 4 + d, 4), c)

    pair = (s, z, y, 1 - c)

    def peer1(k):
        t = lax.rem(me + k, 8)
        return t // 2, lax.rem(t, 2)

    def dev2(k):
        t = lax.rem(place + k, 32)
        return (s, t // 4, lax.rem(t, 4), c)

    barrier = pltpu.get_barrier_semaphore()
    for k in range(1, 8):
        px, pc = peer1(k)
        pl.semaphore_signal(barrier, inc=1, device_id=(px, z, y, pc), device_id_type=MESH)

    def greet(k, carry):
        pl.semaphore_signal(barrier, inc=1, device_id=dev2(k), device_id_type=MESH)
        return carry

    lax.fori_loop(1, 32, greet, 0)

    def vcopy(i):
        at = pl.ds(pl.multiple_of(i * CHUNK, CHUNK), CHUNK)
        return pltpu.make_async_copy(v_hbm.at[at, :], vbuf.at[at, :], vs.at[i])

    def vstart(i, carry):
        vcopy(i).start()
        return carry

    lax.fori_loop(0, NCHUNK, vstart, 0)

    def wcopy(d):
        return remote(w_ref, wbuf.at[s], ws.at[d], wr.at[d], xdev(d))

    def xcopies(d):
        return [
            remote(a, b.at[s], xs.at[n, d], xr.at[n, d], xdev(d))
            for n, (a, b) in enumerate(((codes, codeg), (bit_ref, bitg), (dests, destg)))
        ]

    def slot(cc, zz, yy):
        return cc * 32 + zz * 4 + yy

    def zat(cc, e):
        if EVENTS[e] is None:
            return z
        way, hop = EVENTS[e]
        return lax.rem(z + 8 + (2 * cc - 1) * (1 - 2 * way) * hop, 8)

    def znext(way):
        return (s, lax.rem(z + 8 + (1 - 2 * c) * (1 - 2 * way), 8), y, c)

    def event_of(way, hop):
        return EVENTS.index((way, hop)) if hop else 0

    def part_a(cc, zz, yy):
        return tabs.at[slot(cc, zz, yy), pl.ds(0, A_ROWS), :]

    def part_b(cc, zz):
        return tabs.at[pl.ds(slot(cc, zz, 0), 4), pl.ds(A_ROWS, 256 - A_ROWS), :]

    def yof(d):
        return lax.rem(y + 4 + d, 4)

    def azcopy(way, hop):
        here = part_a(c, zat(c, event_of(way, hop - 1)), y)
        return remote(here, here, azs.at[way, hop], azr.at[way, hop], znext(way))

    def bzcopy(way, hop):
        here = part_b(c, zat(c, event_of(way, hop - 1)))
        return remote(here, here, bzs.at[way, hop], bzr.at[way, hop], znext(way))

    def bycopy(j):
        here = tabs.at[slot(c, z, y), pl.ds(A_ROWS, 256 - A_ROWS), :]
        return remote(here, here, bys.at[j], byr.at[j], ydev((1, -1, 2)[j]))

    def ycopy(k, e):
        here = part_a(c, zat(c, e), y)
        return remote(here, here, ys.at[k, e], yr.at[k, e], ydev(1 - 2 * k))

    def lcopy(e):
        sign = 1 - 2 * (e % 2)
        here = part_a(c, zat(c, e), yof(-sign))
        return remote(here, here, ls.at[e], lr.at[e], ydev(sign))

    def ccopy(k, e, cc):
        here = part_a(cc, zat(cc, e), yof((0, -1, 1, 2)[k]))
        return remote(here, here, cs.at[k, e], cr.at[k, e], pair)

    def cbcopy(e, cc):
        here = part_b(cc, zat(cc, e))
        return remote(here, here, cbs.at[e], cbr.at[e], pair)

    def on_b0():
        for j in range(3):
            bycopy(j).wait_recv()
        bzcopy(0, 1).start()
        bzcopy(1, 1).start()
        cbcopy(0, c).start()

    def on_a(e):
        way, hop = EVENTS[e]
        azcopy(way, hop).wait_recv()
        if hop < HOPS[way]:
            azcopy(way, hop + 1).start()
        ycopy(0, e).start()
        ycopy(1, e).start()
        ccopy(0, e, c).start()

    def on_b(e):
        way, hop = EVENTS[e]
        bzcopy(way, hop).wait_recv()
        if hop < HOPS[way]:
            bzcopy(way, hop + 1).start()
        cbcopy(e, c).start()

    def on_y(e):
        ycopy(0, e).wait_recv()
        ycopy(1, e).wait_recv()
        lcopy(e).start()
        ccopy(1, e, c).start()
        ccopy(2, e, c).start()

    def on_l(e):
        lcopy(e).wait_recv()
        ccopy(3, e, c).start()

    def pcopy(d, i):
        at = pl.ds(pl.multiple_of(i * CHUNK, CHUNK), CHUNK)
        return remote(
            sendbuf.at[lax.rem(s + d, 4), :, at], rbuf.at[s, :, at], ps.at[d, i], pr.at[d, i], xdev(d)
        )

    def put_table(value):
        tabs[slot(c, z, y)] = value

    pl.semaphore_wait(barrier, 38)
    for d in (1, 3, 2):
        wcopy(d).start()
    build_table(s, bk_ref, bv_ref, put_table)

    for j in range(3):
        bycopy(j).start()
    azcopy(0, 1).start()
    azcopy(1, 1).start()
    for k in (0, 1):
        ycopy(k, 0).start()
    ccopy(0, 0, c).start()

    for i in range(NCHUNK):
        at = slice((i % 8) * CHUNK, (i % 8 + 1) * CHUNK)
        m = slice(i // 8, i // 8 + 1)
        codes[i : i + 1, :] = key_ref[m, at] | (grp_ref[m, at] << 11)
    d = dst_ref[...]
    dests[...] = jnp.zeros_like(dests)
    dests[0:2, 0:64] = (d & 1) * 32 + (d >> 3) * 4 + ((d >> 1) & 3)

    for d in (1, 3, 2):
        for cp in xcopies(d):
            cp.start()
    own = [
        pltpu.make_async_copy(a, b.at[s], own_sem.at[n])
        for n, (a, b) in enumerate(((codes, codeg), (bit_ref, bitg), (dests, destg)))
    ]
    for cp in own:
        cp.start()
    half[0] = (0.5 * w_ref[...].astype(F32)).astype(BF16)

    def first_section(i, carry):
        at = pl.ds(pl.multiple_of(i * CHUNK, CHUNK), CHUNK)
        vcopy(i).wait()
        v = vbuf[at, :]
        vbuf[at, :] = silu_add(v.astype(F32), jnp.dot(v, half[0], preferred_element_type=F32))
        return carry

    lax.fori_loop(0, NCHUNK, first_section, 0)
    on_b0()
    on_a(1)
    on_a(2)
    for d in (1, 2, 3):
        wcopy(d).wait_recv()
    for j in (1, 2):
        half[j] = (0.5 * wbuf[lax.rem(s + j, 4)].astype(F32)).astype(BF16)
    last[pl.ds(0, 128), :] = (0.5 * wbuf[lax.rem(s + 3, 4)].astype(F32)).T.astype(BF16)
    eye = lax.broadcasted_iota(jnp.int32, (128, 128), 0) == lax.broadcasted_iota(jnp.int32, (128, 128), 1)
    last[pl.ds(128, 128), :] = eye.astype(F32).astype(BF16)

    def sections(i):
        at = pl.ds(pl.multiple_of(i * CHUNK, CHUNK), CHUNK)
        v = vbuf[at, :]
        for j in (1, 2):
            v = silu_add(v.astype(F32), jnp.dot(v, half[j], preferred_element_type=F32))
        out = lax.dot_general(last[...], v, NT, preferred_element_type=F32)
        v = silu_add(out[128:], out[:128])
        for q in range(4):
            sendbuf[q, :, at] = v[q * COLS : (q + 1) * COLS]

    sections(0)
    during = {
        1: [(on_y, 0)],
        6: [(on_l, 0)],
        7: [(on_a, 3), (on_a, 4)],
        8: [(on_b, 1), (on_b, 2)],
        10: [(on_y, 1), (on_y, 2)],
        14: [(on_a, 5), (on_a, 6)],
        15: [(on_l, 1), (on_l, 2)],
    }

    def step(i, carry):
        sections(i)
        for d in (1, 3, 2):
            pcopy(d, i - 1).start()
        for at, todo in during.items():

            @pl.when(i == at)
            def _(todo=todo):
                for act, e in todo:
                    act(e)

        return carry

    lax.fori_loop(1, NCHUNK, step, 0)
    own_p = pltpu.make_async_copy(sendbuf.at[s], rbuf.at[s], own_sem.at[4])
    own_p.start()
    for d in (1, 3, 2):
        pcopy(d, NCHUNK - 1).start()
    on_b(3)
    on_b(4)
    on_y(3)
    on_y(4)
    on_a(7)

    for cp in own:
        cp.wait()
    for d in (1, 2, 3):
        for cp in xcopies(d):
            cp.wait_recv()
    to_scalar = pltpu.make_async_copy(destg, where_ref, own_sem.at[5])
    to_scalar.start()
    words = bitg[0] & bitg[1] & bitg[2] & bitg[3]
    parts = jnp.concatenate([words & 255, words >> 8], axis=0).astype(F32).astype(BF16)
    shift = lax.broadcasted_iota(jnp.int32, (8, CHUNK), 1) & 15
    wide_iota = lax.broadcasted_iota(jnp.int32, (512, CHUNK), 1) >> 4
    word_iota = lax.broadcasted_iota(jnp.int32, (512, CHUNK), 0)
    for k in range(8):
        spread = (wide_iota + k * 64 == word_iota).astype(F32).astype(BF16)
        got = jnp.dot(parts, spread, preferred_element_type=F32).astype(jnp.int32)
        kept_ref[k] = ((got[:8] + got[8:] * 256) >> shift) & 1
    to_scalar.wait()
    own_p.wait()
    acc_ref[...] = jnp.zeros_like(acc_ref)
    on_l(3)
    on_l(4)
    on_b(5)
    on_b(6)
    on_y(5)
    on_y(6)
    on_l(5)
    on_l(6)
    on_b(7)
    on_y(7)
    on_l(7)
    for e in range(8):
        for k in range(4):
            ccopy(k, e, 1 - c).wait_recv()
        cbcopy(e, 1 - c).wait_recv()

    one, zero = jnp.ones((), BF16), jnp.zeros((), BF16)
    rows256 = lax.broadcasted_iota(jnp.int32, (256, 128), 0).astype(F32).astype(BF16)
    rows128 = lax.broadcasted_iota(jnp.int32, (128, 128), 0).astype(F32).astype(BF16)

    def permuted(entry, code):
        lane = jnp.broadcast_to(code & 127, (8, 128))
        part = jnp.broadcast_to((code >> 7) & 15, (8, 128))
        here = [part == p for p in range(16)]
        got = []
        for r in range(0, COLS, 16):
            for p in range(16):
                rows = slice(p // 2 * COLS + r, p // 2 * COLS + r + 16)
                tile = tabs[entry, rows, p % 2 * 128 : p % 2 * 128 + 128].astype(F32)
                new = [jnp.take_along_axis(tile[h : h + 8], lane, axis=1) for h in (0, 8)]
                held = new if p == 0 else [jnp.where(here[p], n, o) for n, o in zip(new, held)]
            got += held
        return jnp.concatenate(got, axis=0)

    def join_chunk(src, i):
        code = codeg[src, pl.ds(i, 1), :]
        kept = kept_ref[i % 8, pl.ds(2 * src + i // 8, 1), :]
        low = (code & 255).astype(F32).astype(BF16)
        high = (code >> 8) & 7
        glow = (code >> 11) & 7
        ghigh = jnp.where(kept == 1, code >> 14, -1).astype(F32).astype(BF16)
        wide, hots = [], []
        for b in range(CHUNK // 128):
            at = slice(b * 128, (b + 1) * 128)
            entry = where_ref[src, i // 8, (i % 8) * 8 + b]
            if b < PERMUTED:
                matched = permuted(entry, code[:, at])
            else:
                hot = jnp.where(rows256 == low[:, at], one, zero)
                out = jnp.dot(tabs[entry], hot, preferred_element_type=F32)
                matched = jnp.zeros((COLS, 128), F32)
                for p in range(8):
                    matched = jnp.where(high[:, at] == p, out[p * COLS : (p + 1) * COLS], matched)
            pay = rbuf[src, :, pl.ds(pl.multiple_of(i * CHUNK + b * 128, 128), 128)]
            joined = pay.astype(F32) * matched
            wide.append(
                jnp.concatenate(
                    [jnp.where(glow[:, at] == p, joined, 0.0).astype(BF16) for p in range(8)], axis=0
                )
            )
            hots.append(jnp.where(rows128 == ghigh[:, at], one, zero))
        acc_ref[...] += lax.dot_general(
            jnp.concatenate(hots, axis=1), jnp.concatenate(wide, axis=1), NT, preferred_element_type=F32
        )

    def join(i, carry):
        for d in (1, 2, 3):
            pcopy(d, i).wait_recv()
        for d in range(4):
            join_chunk(lax.rem(s + 4 - d, 4), i)
        return carry

    lax.fori_loop(0, NCHUNK, join, 0)

    def piece(px, pc):
        return (
            pl.ds(pl.multiple_of(px * 32, 32), 32),
            pl.ds(pl.multiple_of(pc * 128, 128), 128),
        )

    def copy1(k):
        px, pc = peer1(k)
        rows, lanes = piece(px, pc)
        return remote(acc_ref.at[rows, lanes], first.at[me], s1.at[k], r1.at[k], (px, z, y, pc))

    def copy2(k):
        return remote(mid.at[lax.rem(place + k, 32)], second.at[place], s2.at[k], r2.at[k], dev2(k))

    for k in range(1, 8):
        copy1(k).start()
    rows, lanes = piece(s, c)
    first[me] = acc_ref[rows, lanes]

    for e in range(8):
        for k in range(4):
            ccopy(k, e, c).wait_send()
        cbcopy(e, c).wait_send()
        for k in (0, 1):
            ycopy(k, e).wait_send()
        lcopy(e).wait_send()
    for way in (0, 1):
        for hop in range(1, HOPS[way] + 1):
            azcopy(way, hop).wait_send()
            bzcopy(way, hop).wait_send()
    for j in range(3):
        bycopy(j).wait_send()

    def sent_p(i, carry):
        for d in (1, 2, 3):
            pcopy(d, i).wait_send()
        return carry

    lax.fori_loop(0, NCHUNK, sent_p, 0)
    for d in (1, 2, 3):
        wcopy(d).wait_send()
        for cp in xcopies(d):
            cp.wait_send()

    for k in range(1, 8):
        copy1(k).wait_recv()
    for x in range(4):
        mid[:, x, :] = first[2 * x] + first[2 * x + 1]

    def send(k, carry):
        copy2(k).start()
        return carry

    lax.fori_loop(1, 32, send, 0)
    second[place] = mid[place]

    def take(k, carry):
        copy2(k).wait_recv()
        return carry

    lax.fori_loop(1, 32, take, 0)
    total = jnp.sum(second[...], axis=0)
    for x in range(4):
        for k in range(4):
            out_ref[k : k + 1, x * COLS : (x + 1) * COLS] = total[x : x + 1, k * COLS : (k + 1) * COLS]
    for k in range(1, 8):
        copy1(k).wait_send()

    def done(k, carry):
        copy2(k).wait_send()
        return carry

    lax.fori_loop(1, 32, done, 0)


def local(probe_values, probe_keys, group_ids, block_dest, filter_bits, section_weights, build_keys, build_values):
    dma = pltpu.SemaphoreType.DMA
    vmem = pl.BlockSpec(memory_space=pltpu.VMEM)
    i32 = jnp.int32
    return pl.pallas_call(
        fused_kernel,
        name="fused",
        out_shape=jax.ShapeDtypeStruct((4, 128), F32),
        in_specs=[vmem, pl.BlockSpec(memory_space=pl.ANY)] + [vmem] * 6,
        out_specs=vmem,
        scratch_shapes=[
            pltpu.VMEM((ROWS, 128), BF16),
            pltpu.VMEM((4, COLS, ROWS), BF16),
            pltpu.VMEM((4, COLS, ROWS), BF16),
            pltpu.VMEM((64, 256, 256), BF16),
            pltpu.VMEM((4, 128, 128), BF16),
            pltpu.VMEM((3, 128, 128), BF16),
            pltpu.VMEM((256, 128), BF16),
            pltpu.VMEM((NCHUNK, CHUNK), i32),
            pltpu.VMEM((4, NCHUNK, CHUNK), i32),
            pltpu.VMEM((4, 8, 512), i32),
            pltpu.VMEM((8, 128), i32),
            pltpu.VMEM((4, 8, 128), i32),
            pltpu.SMEM((4, 8, 128), i32),
            pltpu.VMEM((8, 8, CHUNK), i32),
            pltpu.VMEM((128, 256), F32),
            pltpu.VMEM((8, 32, 128), F32),
            pltpu.VMEM((32, 4, 128), F32),
            pltpu.VMEM((32, 4, 128), F32),
            dma((NCHUNK,)),
            dma((4,)), dma((4,)), dma((3, 4)), dma((3, 4)),
            dma((2, 5)), dma((2, 5)), dma((2, 5)), dma((2, 5)), dma((3,)), dma((3,)),
            dma((2, 8)), dma((2, 8)), dma((8,)), dma((8,)),
            dma((4, 8)), dma((4, 8)), dma((8,)), dma((8,)),
            dma((4, NCHUNK)), dma((4, NCHUNK)),
            dma((6,)),
            dma((8,)), dma((8,)), dma((32,)), dma((32,)),
        ],
        compiler_params=pltpu.CompilerParams(
            collective_id=0, has_side_effects=True, vmem_limit_bytes=60 << 20
        ),
    )(
        section_weights[0],
        probe_values.reshape(ROWS, 128),
        probe_keys,
        group_ids,
        block_dest.reshape(2, 64),
        filter_bits[0],
        build_keys.reshape(1, BUILD),
        build_values,
    )


def solution(mesh):
    torus = Mesh(mesh.devices.reshape(mesh.shape["section"], 8, 4, 2), AXES)
    return jax.shard_map(
        local,
        mesh=torus,
        in_specs=(
            P("section", OWNER, None),
            P("section", OWNER),
            P("section", OWNER),
            P("section", OWNER, None),
            P("section", None, OWNER),
            P("section", None, None),
            P(OWNER),
            P(OWNER, None),
        ),
        out_specs=P(AXES, None),
        check_vma=False,
    )
```

```python
import functools

import jax
import jax.numpy as jnp
from jax import lax
from jax.experimental import pallas as pl
from jax.experimental.pallas import tpu as pltpu
from jax.sharding import Mesh
from jax.sharding import PartitionSpec as P

OWNER = ("owner_0", "owner_1", "owner_2")
AXES = ("section", "owner_0", "owner_1", "owner_2")
MESH = pl.DeviceIdType.MESH
F32 = jnp.float32
BF16 = jnp.bfloat16
ROWS = 16384
COLS = 32
CHUNK = 1024
NCHUNK = ROWS // CHUNK
BUILD = 4096
PERMUTED = 4
EARLY = 6
A_ROWS = 176
HOPS = (4, 3)
EVENTS = (None, (0, 1), (1, 1), (0, 2), (1, 2), (0, 3), (1, 3), (0, 4))
NT = (((1,), (1,)), ((), ()))


def remote(src, dst, ssem, rsem, dev):
    return pltpu.make_async_remote_copy(
        src_ref=src, dst_ref=dst, send_sem=ssem, recv_sem=rsem, device_id=dev, device_id_type=MESH
    )


def silu_add(v, h):
    return (v + (h + h * jnp.tanh(h))).astype(BF16)


def build_table(s, bk_ref, bv_ref, store):
    sel = lax.broadcasted_iota(jnp.int32, (COLS, 128), 1) == (
        lax.broadcasted_iota(jnp.int32, (COLS, 128), 0) + s * COLS
    )
    sel = sel.astype(F32).astype(BF16)
    total = jnp.zeros((256, 256), F32)
    step = 1024
    for i in range(BUILD // step):
        vals = lax.dot_general(sel, bv_ref[pl.ds(i * step, step), :], NT, preferred_element_type=F32)
        key = bk_ref[:, pl.ds(i * step, step)]
        low = (key & 255).astype(F32).astype(BF16)
        high = key >> 8
        hot = jnp.where(
            lax.broadcasted_iota(jnp.int32, (256, step), 0).astype(F32).astype(BF16) == low,
            jnp.ones((), BF16),
            jnp.zeros((), BF16),
        )
        wide = jnp.concatenate([jnp.where(high == p, vals, 0.0) for p in range(8)], axis=0)
        total += lax.dot_general(wide.astype(BF16), hot, NT, preferred_element_type=F32)
    store(total.astype(BF16))


def fused_kernel(
    w_ref, v_hbm, key_ref, grp_ref, dst_ref, bit_ref, bk_ref, bv_hbm, out_ref,
    vbuf, bv_ref, sendbuf, rbuf, tabs, wbuf, half, last, codes, codeg, bitg, dests, destg, where_ref, kept_ref,
    acc_ref, first, mid, second,
    vs, ws, wr, xs, xr, azs, azr, bzs, bzr, bys, byr, ys, yr, ls, lr, cs, cr, cbs, cbr, ps, pr, own_sem, s1, r1, s2, r2,
):
    s, z, y, c = [lax.axis_index(a) for a in AXES]
    me = s * 2 + c
    place = z * 4 + y

    def xdev(d):
        return (lax.rem(s + d, 4), z, y, c)

    def ydev(d):
        return (s, z, lax.rem(y + 4 + d, 4), c)

    pair = (s, z, y, 1 - c)

    def peer1(k):
        t = lax.rem(me + k, 8)
        return t // 2, lax.rem(t, 2)

    def dev2(k):
        t = lax.rem(place + k, 32)
        return (s, t // 4, lax.rem(t, 4), c)

    barrier = pltpu.get_barrier_semaphore()
    for k in range(1, 8):
        px, pc = peer1(k)
        pl.semaphore_signal(barrier, inc=1, device_id=(px, z, y, pc), device_id_type=MESH)

    def greet(k, carry):
        pl.semaphore_signal(barrier, inc=1, device_id=dev2(k), device_id_type=MESH)
        return carry

    lax.fori_loop(1, 32, greet, 0)

    def vcopy(i):
        at = pl.ds(pl.multiple_of(i * CHUNK, CHUNK), CHUNK)
        return pltpu.make_async_copy(v_hbm.at[at, :], vbuf.at[at, :], vs.at[i])

    def vstart(i, carry):
        vcopy(i).start()
        return carry

    bv_copy = pltpu.make_async_copy(bv_hbm, bv_ref, own_sem.at[3])
    bv_copy.start()
    lax.fori_loop(0, NCHUNK, vstart, 0)

    def wcopy(d):
        return remote(w_ref, wbuf.at[s], ws.at[d], wr.at[d], xdev(d))

    def xcopies(d):
        return [
            remote(a, b.at[s], xs.at[n, d], xr.at[n, d], xdev(d))
            for n, (a, b) in enumerate(((codes, codeg), (bit_ref, bitg), (dests, destg)))
        ]

    def slot(cc, zz, yy):
        return cc * 32 + zz * 4 + yy

    def zat(cc, e):
        if EVENTS[e] is None:
            return z
        way, hop = EVENTS[e]
        return lax.rem(z + 8 + (2 * cc - 1) * (1 - 2 * way) * hop, 8)

    def znext(way):
        return (s, lax.rem(z + 8 + (1 - 2 * c) * (1 - 2 * way), 8), y, c)

    def event_of(way, hop):
        return EVENTS.index((way, hop)) if hop else 0

    def part_a(cc, zz, yy):
        return tabs.at[slot(cc, zz, yy), pl.ds(0, A_ROWS), :]

    def part_b(cc, zz):
        return tabs.at[pl.ds(slot(cc, zz, 0), 4), pl.ds(A_ROWS, 256 - A_ROWS), :]

    def yof(d):
        return lax.rem(y + 4 + d, 4)

    def azcopy(way, hop):
        here = part_a(c, zat(c, event_of(way, hop - 1)), y)
        return remote(here, here, azs.at[way, hop], azr.at[way, hop], znext(way))

    def bzcopy(way, hop):
        here = part_b(c, zat(c, event_of(way, hop - 1)))
        return remote(here, here, bzs.at[way, hop], bzr.at[way, hop], znext(way))

    def bycopy(j):
        here = tabs.at[slot(c, z, y), pl.ds(A_ROWS, 256 - A_ROWS), :]
        return remote(here, here, bys.at[j], byr.at[j], ydev((1, -1, 2)[j]))

    def ycopy(k, e):
        here = part_a(c, zat(c, e), y)
        return remote(here, here, ys.at[k, e], yr.at[k, e], ydev(1 - 2 * k))

    def lcopy(e):
        sign = 1 - 2 * (e % 2)
        here = part_a(c, zat(c, e), yof(-sign))
        return remote(here, here, ls.at[e], lr.at[e], ydev(sign))

    def ccopy(k, e, cc):
        here = part_a(cc, zat(cc, e), yof((0, -1, 1, 2)[k]))
        return remote(here, here, cs.at[k, e], cr.at[k, e], pair)

    def cbcopy(e, cc):
        here = part_b(cc, zat(cc, e))
        return remote(here, here, cbs.at[e], cbr.at[e], pair)

    def on_b0():
        for j in range(3):
            bycopy(j).wait_recv()
        bzcopy(0, 1).start()
        bzcopy(1, 1).start()
        cbcopy(0, c).start()

    def on_a(e):
        way, hop = EVENTS[e]
        azcopy(way, hop).wait_recv()
        if hop < HOPS[way]:
            azcopy(way, hop + 1).start()
        ycopy(0, e).start()
        ycopy(1, e).start()
        ccopy(0, e, c).start()

    def on_b(e):
        way, hop = EVENTS[e]
        bzcopy(way, hop).wait_recv()
        if hop < HOPS[way]:
            bzcopy(way, hop + 1).start()
        cbcopy(e, c).start()

    def on_y(e):
        ycopy(0, e).wait_recv()
        ycopy(1, e).wait_recv()
        lcopy(e).start()
        ccopy(1, e, c).start()
        ccopy(2, e, c).start()

    def on_l(e):
        lcopy(e).wait_recv()
        ccopy(3, e, c).start()

    def pcopy(d, i):
        at = pl.ds(pl.multiple_of(i * CHUNK, CHUNK), CHUNK)
        return remote(
            sendbuf.at[lax.rem(s + d, 4), :, at], rbuf.at[s, :, at], ps.at[d, i], pr.at[d, i], xdev(d)
        )

    def put_table(value):
        tabs[slot(c, z, y)] = value

    pl.semaphore_wait(barrier, 38)
    for d in (1, 3, 2):
        wcopy(d).start()
    bv_copy.wait()
    build_table(s, bk_ref, bv_ref, put_table)

    for j in range(3):
        bycopy(j).start()
    azcopy(0, 1).start()
    azcopy(1, 1).start()
    for k in (0, 1):
        ycopy(k, 0).start()
    ccopy(0, 0, c).start()

    for i in range(NCHUNK):
        at = slice((i % 8) * CHUNK, (i % 8 + 1) * CHUNK)
        m = slice(i // 8, i // 8 + 1)
        codes[i : i + 1, :] = key_ref[m, at] | (grp_ref[m, at] << 11)
    d = dst_ref[...]
    dests[...] = jnp.zeros_like(dests)
    dests[0:2, 0:64] = (d & 1) * 32 + (d >> 3) * 4 + ((d >> 1) & 3)

    for d in (1, 3, 2):
        for cp in xcopies(d):
            cp.start()
    own = [
        pltpu.make_async_copy(a, b.at[s], own_sem.at[n])
        for n, (a, b) in enumerate(((codes, codeg), (bit_ref, bitg), (dests, destg)))
    ]
    for cp in own:
        cp.start()
    half[0] = (0.5 * w_ref[...].astype(F32)).astype(BF16)

    def first_section(i, carry):
        at = pl.ds(pl.multiple_of(i * CHUNK, CHUNK), CHUNK)
        vcopy(i).wait()
        v = vbuf[at, :]
        vbuf[at, :] = silu_add(v.astype(F32), jnp.dot(v, half[0], preferred_element_type=F32))
        return carry

    lax.fori_loop(0, EARLY, first_section, 0)
    on_b0()
    on_a(1)
    on_a(2)
    for d in (1, 2, 3):
        wcopy(d).wait_recv()
    for j in (1, 2):
        half[j] = (0.5 * wbuf[lax.rem(s + j, 4)].astype(F32)).astype(BF16)
    last[pl.ds(0, 128), :] = (0.5 * wbuf[lax.rem(s + 3, 4)].astype(F32)).T.astype(BF16)
    eye = lax.broadcasted_iota(jnp.int32, (128, 128), 0) == lax.broadcasted_iota(jnp.int32, (128, 128), 1)
    last[pl.ds(128, 128), :] = eye.astype(F32).astype(BF16)

    def sections(i, todo):
        at = pl.ds(pl.multiple_of(i * CHUNK, CHUNK), CHUNK)
        if 0 in todo:
            vcopy(i).wait()
        v = vbuf[at, :]
        for j in todo:
            v = silu_add(v.astype(F32), jnp.dot(v, half[j], preferred_element_type=F32))
        out = lax.dot_general(last[...], v, NT, preferred_element_type=F32)
        v = silu_add(out[128:], out[:128])
        for q in range(4):
            sendbuf[q, :, at] = v[q * COLS : (q + 1) * COLS]

    sections(0, (1, 2))
    during = {
        1: [(on_y, 0)],
        2: [(on_a, 3), (on_a, 4)],
        4: [(on_y, 1), (on_y, 2)],
        5: [(on_l, 0)],
        6: [(on_b, 1), (on_b, 2)],
        8: [(on_a, 5), (on_a, 6)],
        9: [(on_l, 1), (on_l, 2)],
        10: [(on_y, 3), (on_y, 4)],
        11: [(on_b, 3), (on_b, 4)],
        12: [(on_a, 7)],
        13: [(on_l, 3), (on_l, 4)],
        14: [(on_y, 5), (on_y, 6)],
        15: [(on_b, 5), (on_b, 6)],
    }

    def step(i, carry, first, sections_left):
        sections(i, sections_left)
        for d in (1, 3, 2):
            pcopy(d, i - 1).start()
        for at, todo in during.items():
            if (at < EARLY) != first:
                continue

            @pl.when(i == at)
            def _(todo=todo):
                for act, e in todo:
                    act(e)

        return carry

    lax.fori_loop(1, EARLY, functools.partial(step, first=True, sections_left=(1, 2)), 0)
    lax.fori_loop(EARLY, NCHUNK, functools.partial(step, first=False, sections_left=(0, 1, 2)), 0)
    own_p = pltpu.make_async_copy(sendbuf.at[s], rbuf.at[s], own_sem.at[4])
    own_p.start()
    for d in (1, 3, 2):
        pcopy(d, NCHUNK - 1).start()
    on_y(7)

    for cp in own:
        cp.wait()
    for d in (1, 2, 3):
        for cp in xcopies(d):
            cp.wait_recv()
    to_scalar = pltpu.make_async_copy(destg, where_ref, own_sem.at[5])
    to_scalar.start()
    words = bitg[0] & bitg[1] & bitg[2] & bitg[3]
    parts = jnp.concatenate([words & 255, words >> 8], axis=0).astype(F32).astype(BF16)
    shift = lax.broadcasted_iota(jnp.int32, (8, CHUNK), 1) & 15
    wide_iota = lax.broadcasted_iota(jnp.int32, (512, CHUNK), 1) >> 4
    word_iota = lax.broadcasted_iota(jnp.int32, (512, CHUNK), 0)
    for k in range(8):
        spread = (wide_iota + k * 64 == word_iota).astype(F32).astype(BF16)
        got = jnp.dot(parts, spread, preferred_element_type=F32).astype(jnp.int32)
        kept_ref[k] = ((got[:8] + got[8:] * 256) >> shift) & 1
    to_scalar.wait()
    own_p.wait()
    acc_ref[...] = jnp.zeros_like(acc_ref)
    on_l(5)
    on_l(6)
    on_l(7)
    on_b(7)
    for e in range(8):
        for k in range(4):
            ccopy(k, e, 1 - c).wait_recv()
        cbcopy(e, 1 - c).wait_recv()

    one, zero = jnp.ones((), BF16), jnp.zeros((), BF16)
    rows256 = lax.broadcasted_iota(jnp.int32, (256, 128), 0).astype(F32).astype(BF16)
    rows128 = lax.broadcasted_iota(jnp.int32, (128, 128), 0).astype(F32).astype(BF16)

    def permuted(entry, code):
        lane = jnp.broadcast_to(code & 127, (8, 128))
        part = jnp.broadcast_to((code >> 7) & 15, (8, 128))
        here = [part == p for p in range(16)]
        got = []
        for r in range(0, COLS, 16):
            for p in range(16):
                rows = slice(p // 2 * COLS + r, p // 2 * COLS + r + 16)
                tile = tabs[entry, rows, p % 2 * 128 : p % 2 * 128 + 128].astype(F32)
                new = [jnp.take_along_axis(tile[h : h + 8], lane, axis=1) for h in (0, 8)]
                held = new if p == 0 else [jnp.where(here[p], n, o) for n, o in zip(new, held)]
            got += held
        return jnp.concatenate(got, axis=0)

    def join_chunk(src, i):
        code = codeg[src, pl.ds(i, 1), :]
        kept = kept_ref[i % 8, pl.ds(2 * src + i // 8, 1), :]
        low = (code & 255).astype(F32).astype(BF16)
        high = (code >> 8) & 7
        glow = (code >> 11) & 7
        ghigh = jnp.where(kept == 1, code >> 14, -1).astype(F32).astype(BF16)
        wide, hots = [], []
        for b in range(CHUNK // 128):
            at = slice(b * 128, (b + 1) * 128)
            entry = where_ref[src, i // 8, (i % 8) * 8 + b]
            if b < PERMUTED:
                matched = permuted(entry, code[:, at])
            else:
                hot = jnp.where(rows256 == low[:, at], one, zero)
                out = jnp.dot(tabs[entry], hot, preferred_element_type=F32)
                matched = jnp.zeros((COLS, 128), F32)
                for p in range(8):
                    matched = jnp.where(high[:, at] == p, out[p * COLS : (p + 1) * COLS], matched)
            pay = rbuf[src, :, pl.ds(pl.multiple_of(i * CHUNK + b * 128, 128), 128)]
            joined = pay.astype(F32) * matched
            wide.append(
                jnp.concatenate(
                    [jnp.where(glow[:, at] == p, joined, 0.0).astype(BF16) for p in range(8)], axis=0
                )
            )
            hots.append(jnp.where(rows128 == ghigh[:, at], one, zero))
        acc_ref[...] += lax.dot_general(
            jnp.concatenate(hots, axis=1), jnp.concatenate(wide, axis=1), NT, preferred_element_type=F32
        )

    def join(i, carry):
        for d in (1, 2, 3):
            pcopy(d, i).wait_recv()
        for d in range(4):
            join_chunk(lax.rem(s + 4 - d, 4), i)
        return carry

    lax.fori_loop(0, NCHUNK, join, 0)

    def piece(px, pc):
        return (
            pl.ds(pl.multiple_of(px * 32, 32), 32),
            pl.ds(pl.multiple_of(pc * 128, 128), 128),
        )

    def copy1(k):
        px, pc = peer1(k)
        rows, lanes = piece(px, pc)
        return remote(acc_ref.at[rows, lanes], first.at[me], s1.at[k], r1.at[k], (px, z, y, pc))

    def copy2(k):
        return remote(mid.at[lax.rem(place + k, 32)], second.at[place], s2.at[k], r2.at[k], dev2(k))

    for k in range(1, 8):
        copy1(k).start()
    rows, lanes = piece(s, c)
    first[me] = acc_ref[rows, lanes]

    for e in range(8):
        for k in range(4):
            ccopy(k, e, c).wait_send()
        cbcopy(e, c).wait_send()
        for k in (0, 1):
            ycopy(k, e).wait_send()
        lcopy(e).wait_send()
    for way in (0, 1):
        for hop in range(1, HOPS[way] + 1):
            azcopy(way, hop).wait_send()
            bzcopy(way, hop).wait_send()
    for j in range(3):
        bycopy(j).wait_send()

    def sent_p(i, carry):
        for d in (1, 2, 3):
            pcopy(d, i).wait_send()
        return carry

    lax.fori_loop(0, NCHUNK, sent_p, 0)
    for d in (1, 2, 3):
        wcopy(d).wait_send()
        for cp in xcopies(d):
            cp.wait_send()

    for k in range(1, 8):
        copy1(k).wait_recv()
    for x in range(4):
        mid[:, x, :] = first[2 * x] + first[2 * x + 1]

    def send(k, carry):
        copy2(k).start()
        return carry

    lax.fori_loop(1, 32, send, 0)
    second[place] = mid[place]
    for k in range(1, 8):
        copy1(k).wait_send()

    def done(k, carry):
        copy2(k).wait_send()
        return carry

    lax.fori_loop(1, 32, done, 0)

    def take(k, carry):
        copy2(k).wait_recv()
        return carry

    lax.fori_loop(1, 32, take, 0)
    total = jnp.sum(second[...], axis=0)
    for x in range(4):
        for k in range(4):
            out_ref[k : k + 1, x * COLS : (x + 1) * COLS] = total[x : x + 1, k * COLS : (k + 1) * COLS]


def local(probe_values, probe_keys, group_ids, block_dest, filter_bits, section_weights, build_keys, build_values):
    dma = pltpu.SemaphoreType.DMA
    vmem = pl.BlockSpec(memory_space=pltpu.VMEM)
    hbm = pl.BlockSpec(memory_space=pl.ANY)
    i32 = jnp.int32
    return pl.pallas_call(
        fused_kernel,
        name="fused",
        out_shape=jax.ShapeDtypeStruct((4, 128), F32),
        in_specs=[vmem, hbm] + [vmem] * 5 + [hbm],
        out_specs=vmem,
        scratch_shapes=[
            pltpu.VMEM((ROWS, 128), BF16),
            pltpu.VMEM((BUILD, 128), BF16),
            pltpu.VMEM((4, COLS, ROWS), BF16),
            pltpu.VMEM((4, COLS, ROWS), BF16),
            pltpu.VMEM((64, 256, 256), BF16),
            pltpu.VMEM((4, 128, 128), BF16),
            pltpu.VMEM((3, 128, 128), BF16),
            pltpu.VMEM((256, 128), BF16),
            pltpu.VMEM((NCHUNK, CHUNK), i32),
            pltpu.VMEM((4, NCHUNK, CHUNK), i32),
            pltpu.VMEM((4, 8, 512), i32),
            pltpu.VMEM((8, 128), i32),
            pltpu.VMEM((4, 8, 128), i32),
            pltpu.SMEM((4, 8, 128), i32),
            pltpu.VMEM((8, 8, CHUNK), i32),
            pltpu.VMEM((128, 256), F32),
            pltpu.VMEM((8, 32, 128), F32),
            pltpu.VMEM((32, 4, 128), F32),
            pltpu.VMEM((32, 4, 128), F32),
            dma((NCHUNK,)),
            dma((4,)), dma((4,)), dma((3, 4)), dma((3, 4)),
            dma((2, 5)), dma((2, 5)), dma((2, 5)), dma((2, 5)), dma((3,)), dma((3,)),
            dma((2, 8)), dma((2, 8)), dma((8,)), dma((8,)),
            dma((4, 8)), dma((4, 8)), dma((8,)), dma((8,)),
            dma((4, NCHUNK)), dma((4, NCHUNK)),
            dma((6,)),
            dma((8,)), dma((8,)), dma((32,)), dma((32,)),
        ],
        compiler_params=pltpu.CompilerParams(
            collective_id=0, has_side_effects=True, vmem_limit_bytes=60 << 20
        ),
    )(
        section_weights[0],
        probe_values.reshape(ROWS, 128),
        probe_keys,
        group_ids,
        block_dest.reshape(2, 64),
        filter_bits[0],
        build_keys.reshape(1, BUILD),
        build_values,
    )


def solution(mesh):
    torus = Mesh(mesh.devices.reshape(mesh.shape["section"], 8, 4, 2), AXES)
    return jax.shard_map(
        local,
        mesh=torus,
        in_specs=(
            P("section", OWNER, None),
            P("section", OWNER),
            P("section", OWNER),
            P("section", OWNER, None),
            P("section", None, OWNER),
            P("section", None, None),
            P(OWNER),
            P(OWNER, None),
        ),
        out_specs=P(AXES, None),
        check_vma=False,
    )
```
